32 devices in a mesh: dp: 8 (over y, x, core), rep: 4 (over z).
Axes of the slice: x: 2, y: 2, z: 4, core: 2. Of those that a mesh axis runs over, the one named last changes fastest.
Arguments:
- tokens: bfloat16 [32768, 768], P(('dp', 'rep')), may hold values from -6 to 6
- query_weight: bfloat16 [768, 768], replicated, may hold values from -0.21875 to 0.21875
- key_weight: bfloat16 [768, 768], replicated, may hold values from -0.21875 to 0.21875
- value_weight: bfloat16 [768, 768], replicated, may hold values from -0.21875 to 0.21875
- output_weight: bfloat16 [768, 768], replicated, may hold values from -0.875 to 0.875
- expand_weight: bfloat16 [768, 3072], replicated, may hold values from -0.21875 to 0.21875
- contract_weight: bfloat16 [3072, 768], replicated, may hold values from -0.109375 to 0.109375
- query_bias: float32 [768], replicated, may hold values from -3 to 3
- value_bias: float32 [768], replicated, may hold values from -3 to 3
- output_bias: float32 [768], replicated, may hold values from -3 to 3
- first_gain: float32 [768], replicated, may hold values from 0.5 to 1.5
- first_shift: float32 [768], replicated, may hold values from -3 to 3
- expand_bias: float32 [3072], replicated, may hold values from -3 to 3
- contract_bias: float32 [768], replicated, may hold values from -3 to 3
- second_gain: float32 [768], replicated, may hold values from 0.5 to 1.5
- second_shift: float32 [768], replicated, may hold values from -3 to 3
- cotangent: bfloat16 [32768, 768], P(('dp', 'rep')), may hold values from -6 to 6
- lengths: int32 [64], P(('dp', 'rep')), may hold values from 256 to 512, as said below
- counts: int32 [32], P(('dp', 'rep')), may hold values from 0 to 2, as said below
Outputs:
- states: bfloat16 [32768, 768], P(('dp', 'rep'))
- grad_tokens: float32 [32768, 768], P(('dp', 'rep'))
- grad_query_weight: float32 [768, 768], replicated
- grad_key_weight: float32 [768, 768], replicated
- grad_value_weight: float32 [768, 768], replicated
- grad_output_weight: float32 [768, 768], replicated
- grad_expand_weight: float32 [768, 3072], replicated
- grad_contract_weight: float32 [3072, 768], replicated
- grad_query_bias: float32 [768], replicated
- grad_value_bias: float32 [768], replicated
- grad_output_bias: float32 [768], replicated
- grad_first_gain: float32 [768], replicated
- grad_first_shift: float32 [768], replicated
- grad_expand_bias: float32 [3072], replicated
- grad_contract_bias: float32 [768], replicated
- grad_second_gain: float32 [768], replicated
- grad_second_shift: float32 [768], replicated
The draws below stay inside these ranges and needn't reach their ends.
Inputs may be any that keep to these rules, and one draw needn't show every extreme that they name: `lengths`: token count of each passage slot; some slot has exactly 512 and some exactly 256. `counts`: the number of leading passage slots of each device that hold a passage; some device holds 2 and some none.
All inputs are finite; a program needn't handle non-finite values.
Results may differ from the reference program's by a relative error of at most 0.014.
Values sent between devices are 32-bit elements; how exact they have to be, the bound alone decides.
No kernel may reach another device: no remote copies, remote signals or barrier semaphores. Data moves between devices by JAX's collectives and lax.ppermute only.
A program may use at most 192 MiB of HBM per device.

```python
import jax
import jax.numpy as jnp
from jax import lax

D = 768
FF = 3072
HEADS = 12
HEAD_DIM = 64
PASSAGE = 512
SLOTS = 2
PASSAGES = 64
TOKENS = 32768
DEVICES = 32


def draw_lengths(key, part):
    drawn = jax.random.randint(key, (PASSAGES,), PASSAGE // 2, PASSAGE + 1)
    drawn = drawn.at[0].set(PASSAGE)
    drawn = drawn.at[1].set(PASSAGE // 2)
    return drawn.astype(jnp.int32)


def draw_counts(key, part):
    drawn = jax.random.randint(key, (DEVICES,), 1, SLOTS + 1)
    drawn = drawn.at[0].set(SLOTS)
    drawn = drawn.at[1].set(SLOTS)
    drawn = drawn.at[2].set(0)
    return drawn.astype(jnp.int32)


def spiked(values, stream_key, source, target, parts, factor):
    def block_of(axis_at):
        return (jnp.arange(values.shape[axis_at]) // (values.shape[axis_at] // parts)).reshape((-1,) + (1,) * (values.ndim - 1 - axis_at))

    near = jax.random.permutation(stream_key, parts)[block_of(target)]
    second = (block_of(target) + parts // 2) % parts
    return jnp.where((block_of(source) == near) | (block_of(source) == second), factor * values, values)


def level_of(rng, dims, cuts, low, largest):
    def one(position, shards_of):
        steps = jax.random.uniform(jax.random.fold_in(jax.random.fold_in(rng, 6), position), (shards_of,), jnp.float32, low / len(cuts), largest / len(cuts))
        return jnp.repeat(jnp.exp(steps), dims[position] // shards_of).reshape((-1,) + (1,) * (len(dims) - position - 1))

    loudness = one(*cuts[0])
    for cut in cuts[1:]:
        loudness = loudness * one(*cut)
    return loudness


def bell_draw(stream_key, shape, spread, bound, cuts=(), kind=jnp.bfloat16):
    level = level_of(stream_key, shape, cuts, -0.22, 0.18) if cuts else 1.0
    entries = jax.random.normal(stream_key, shape, jnp.float32) * spread * level
    return jnp.minimum(jnp.maximum(entries, -bound), bound).astype(kind)


def bell_draw_with(own_key, shape, scale, bound, split, heavy, kind=jnp.bfloat16):
    result = scale * jax.random.normal(own_key, shape, jnp.float32)
    if split:
        result = result * level_of(own_key, shape, split, -0.22, 0.18)
    return jnp.clip(spiked(result, jax.random.fold_in(own_key, 3), *heavy), -bound, bound).astype(kind)


def setup_inputs(seed: int = 0) -> dict:
    streams_of = jax.random.split(jax.random.key(seed), 20)
    return {
        "tokens": bell_draw(streams_of[0], (TOKENS, D), 1.0, 6.0, ((0, 32),)),
        "query_weight": bell_draw(streams_of[1], (D, D), D ** -0.5, 0.21875),
        "key_weight": bell_draw(streams_of[2], (D, D), D ** -0.5, 0.21875),
        "value_weight": bell_draw(streams_of[3], (D, D), D ** -0.5, 0.21875),
        "output_weight": bell_draw(streams_of[4], (D, D), (D // 16) ** -0.5, 0.875),
        "expand_weight": bell_draw(streams_of[5], (D, FF), D ** -0.5, 0.21875),
        "contract_weight": bell_draw(streams_of[6], (FF, D), FF ** -0.5, 0.109375),
        "query_bias": bell_draw(streams_of[7], (D,), 0.5, 3.0, (), jnp.float32),
        "value_bias": bell_draw(streams_of[8], (D,), 0.5, 3.0, (), jnp.float32),
        "output_bias": bell_draw(streams_of[9], (D,), 0.5, 3.0, (), jnp.float32),
        "first_gain": jnp.clip(1.0 + 0.1 * jax.random.normal(streams_of[10], (D,), jnp.float32), 0.5, 1.5),
        "first_shift": bell_draw(streams_of[11], (D,), 0.5, 3.0, (), jnp.float32),
        "expand_bias": bell_draw(streams_of[12], (FF,), 0.5, 3.0, (), jnp.float32),
        "contract_bias": bell_draw(streams_of[13], (D,), 0.5, 3.0, (), jnp.float32),
        "second_gain": jnp.clip(1.0 + 0.1 * jax.random.normal(streams_of[14], (D,), jnp.float32), 0.5, 1.5),
        "second_shift": bell_draw(streams_of[15], (D,), 0.5, 3.0, (), jnp.float32),
        "cotangent": bell_draw_with(streams_of[16], (TOKENS, D), 1.0, 6.0, ((0, 32),), (0, 1, 32, 2.75)),
        "lengths": draw_lengths(jax.random.fold_in(streams_of[19], 71), 0),
        "counts": draw_counts(jax.random.fold_in(streams_of[19], 71), 0),
    }


highest = lax.Precision.HIGHEST
epsilon = 1e-05

@jax.custom_vjp
def low(v):
    return lax.optimization_barrier(v.astype(jnp.bfloat16)).astype(jnp.float32)

@jax.custom_vjp
def low_back(v):
    return v

def low_keep(v):
    return (low(v), None)

def low_pass(kept, grad):
    return (grad,)

def back_keep(v):
    return (v, None)

def back_low(kept, grad):
    return (low(grad),)
low.defvjp(low_keep, low_pass)
low_back.defvjp(back_keep, back_low)

def matmul(left_op, right_op):
    return jnp.dot(left_op, right_op, precision=highest, preferred_element_type=jnp.float32)

def norm_rows(row_block, gain_row, shift_row):
    centred = row_block - lax.optimization_barrier(jnp.mean(row_block, axis=-1, keepdims=True))
    scaled = centred * lax.rsqrt(lax.optimization_barrier(jnp.mean(centred * centred, axis=-1, keepdims=True)) + epsilon)
    return scaled * gain_row + shift_row

def encoder_layer(inputs, params, key_live, live_rows):
    query_weight, key_weight, value_weight, output_weight, expand_weight, contract_weight, query_bias, value_bias, output_bias, first_gain, first_shift, expand_bias, contract_bias, second_gain, second_shift = params
    slot_count, passage_len = key_live.shape
    heads_shape = (slot_count, passage_len, HEADS, HEAD_DIM)
    queries = low(low_back(matmul(inputs, query_weight) + query_bias)).reshape(heads_shape)
    key_rows = low(low_back(matmul(inputs, key_weight))).reshape(heads_shape)
    values = low(low_back(matmul(inputs, value_weight) + value_bias)).reshape(heads_shape)
    scores = jnp.einsum('sqhe,skhe->shqk', queries, key_rows, precision=highest) * 0.125
    scores = low_back(jnp.where(key_live[:, None, None, :] > 0, scores, -1000000000.0))
    attn_probs = low(jax.nn.softmax(scores, axis=-1))
    context = jnp.einsum('shqk,skhe->sqhe', attn_probs, values, precision=highest)
    context = low(low_back(context.reshape(inputs.shape[0], -1)))
    attended = low_back(matmul(context, output_weight) + output_bias)
    first_out = norm_rows(inputs + attended, first_gain, first_shift)
    hidden = low_back(matmul(low(first_out), expand_weight) + expand_bias)
    active = low(jax.nn.gelu(hidden, approximate=False))
    second = low_back(matmul(active, contract_weight) + contract_bias)
    return norm_rows(first_out + second, second_gain, second_shift) * live_rows[:, None]

def add_up(total_a, total_b):
    return total_a + total_b

def reference(tokens, query_weight, key_weight, value_weight, output_weight, expand_weight, contract_weight, query_bias, value_bias, output_bias, first_gain, first_shift, expand_bias, contract_bias, second_gain, second_shift, cotangent, lengths, counts):
    params = (query_weight.astype(jnp.float32), key_weight.astype(jnp.float32), value_weight.astype(jnp.float32), output_weight.astype(jnp.float32), expand_weight.astype(jnp.float32), contract_weight.astype(jnp.float32), query_bias, value_bias, output_bias, first_gain, first_shift, expand_bias, contract_bias, second_gain, second_shift)
    passage_ids = jnp.arange(PASSAGES, dtype=jnp.int32)
    device_ids = (passage_ids // SLOTS).astype(jnp.int32)
    slot_live = passage_ids % SLOTS < counts[device_ids]
    positions = jnp.arange(PASSAGE, dtype=jnp.int32)
    key_live = (positions[None, :] < lengths[:, None]).astype(jnp.float32)
    live_rows = key_live * slot_live[:, None].astype(jnp.float32)
    group_size = min(8, PASSAGES)
    step_count = PASSAGES // group_size
    inputs = tokens.astype(jnp.float32).reshape(step_count, group_size * PASSAGE, D)
    incoming = cotangent.astype(jnp.float32).reshape(step_count, group_size * PASSAGE, D)
    key_groups = key_live.reshape(step_count, group_size, PASSAGE)
    live_groups = live_rows.reshape(step_count, group_size * PASSAGE)

    def one_step(totals, pieces):
        block_in, block_cot, block_keys, block_live = pieces

        def local_layer(layer_in, layer_params):
            return encoder_layer(layer_in, layer_params, block_keys, block_live)
        outputs, pullback = jax.vjp(local_layer, block_in, params)
        grad_in, grad_params = pullback(block_cot)
        totals = jax.tree.map(add_up, totals, grad_params)
        return (totals, (outputs.astype(jnp.bfloat16), grad_in))
    zero_init = jax.tree.map(jnp.zeros_like, params)
    totals, (states, grad_tokens) = lax.scan(one_step, zero_init, (inputs, incoming, key_groups, live_groups))
    return (states.reshape(TOKENS, D), grad_tokens.reshape(TOKENS, D), totals[0], totals[1], totals[2], totals[3], totals[4], totals[5], totals[6], totals[7], totals[8], totals[9], totals[10], totals[11], totals[12], totals[13], totals[14])
```

```python
import jax
import jax.numpy as jnp
from jax import lax
from jax.experimental import pallas as pl
from jax.experimental.pallas import tpu as pltpu
from jax.sharding import PartitionSpec as P

HEAD_DIM = 64


epsilon = 1e-05


def project(left_op, right_op):
    return jnp.dot(left_op, right_op, preferred_element_type=jnp.float32)


def project_left(left_op, right_op):
    return lax.dot_general(
        left_op, right_op, (((0,), (0,)), ((), ())), preferred_element_type=jnp.float32
    )


def project_right(left_op, right_op):
    return lax.dot_general(
        left_op, right_op, (((1,), (1,)), ((), ())), preferred_element_type=jnp.float32
    )


def norm_rows(row_block, gain_row, shift_row):
    centred = row_block - jnp.mean(row_block, axis=-1, keepdims=True)
    inverse = lax.rsqrt(jnp.mean(centred * centred, axis=-1, keepdims=True) + epsilon)
    normed = centred * inverse
    return (normed * gain_row + shift_row, normed, inverse)


def norm_back(grad_rows, normed, inverse, gain_row):
    scaled = grad_rows * gain_row
    grad_in = inverse * (
        scaled
        - jnp.mean(scaled, axis=-1, keepdims=True)
        - normed * jnp.mean(scaled * normed, axis=-1, keepdims=True)
    )
    return (grad_in, jnp.sum(grad_rows * normed, 0), jnp.sum(grad_rows, 0))


def bit_orders(size):
    bits = size.bit_length() - 1
    rest = list(range(1, bits))
    return ([0] + rest, [0] + rest[1:] + rest[:1])


def step_pairs(size, step):
    orders = bit_orders(size)
    return [(i, i ^ (1 << orders[i & 1][step])) for i in range(size)]


def step_side(index, size, step):
    even, odd = bit_orders(size)
    return jnp.where(index & 1, (index >> odd[step]) & 1, (index >> even[step]) & 1)


def dp_steps():
    return lax.axis_size("dp").bit_length() - 1


def rep_steps():
    return lax.axis_size("rep").bit_length() - 1


def my_side(step):
    first = dp_steps()
    if step >= first:
        return (lax.axis_index("rep") >> (step - first)) & 1
    return step_side(lax.axis_index("dp"), lax.axis_size("dp"), step)


def swap(block, step):
    first = dp_steps()
    if step >= first:
        reach = 1 << (step - first)
        return lax.ppermute(
            block, "rep", [(i, i ^ reach) for i in range(lax.axis_size("rep"))]
        )
    return lax.ppermute(block, "dp", step_pairs(lax.axis_size("dp"), step))


def gate(*values):
    return lax.optimization_barrier(values)


def halve(terms, step, small=None):
    kept, swapped = gate(*terms)
    rows = kept.shape[0] // 2
    side = my_side(step)

    def part(which):
        return lax.dynamic_slice_in_dim(kept, which * rows, rows, 0) + (
            lax.dynamic_slice_in_dim(swapped, which * rows, rows, 0)
        )

    sent = part(1 - side)
    if small is not None:
        small = small + swapped[2 * rows :]
        sent = jnp.concatenate([sent, small], 0)
    return (part(side), swap(sent, step)), small


def reduce_rest(terms, first, small=None):
    last = dp_steps() + rep_steps()
    for step in range(first, last):
        terms, small = halve(terms, step, small)
    kept, swapped = gate(*terms)
    rows = kept.shape[0]
    if small is None:
        return kept + swapped
    return kept + swapped[:rows], small + swapped[rows:]


def join(block, swapped, step):
    block, swapped = gate(block, swapped)
    low = my_side(step) == 0
    return jnp.concatenate(
        [jnp.where(low, block, swapped), jnp.where(low, swapped, block)], 0
    )


def spread(block, rows):
    for step in reversed(range(2, dp_steps() + rep_steps())):
        block = join(block, swap(block, step), step)
    size = lax.axis_size("dp")
    index = lax.axis_index("dp")
    other = swap(block, 1)
    pieces = [block, other, swap(block, 0), swap(other, 0)]

    def place(device, step):
        return step_side(device, size, step) * (rows >> (step + 1))

    places = []
    for device in (index, index ^ 1):
        mine = place(device, 1)
        places += [place(device, 0) + mine, place(device, 0) + (rows >> 2) - mine]
    return list(zip(places, pieces))


def blank_kernel(out_ref):
    pass


def blank(shape):
    return pl.pallas_call(
        blank_kernel,
        out_specs=pl.BlockSpec(memory_space=pl.ANY),
        out_shape=jax.ShapeDtypeStruct(shape, jnp.float32),
        name="blank",
    )()


def assemble(pieces, rows):
    whole = blank((rows, pieces[0][1].shape[1]))
    for at, part in pieces:
        whole = lax.dynamic_update_slice_in_dim(whole, part, at, 0)
    return whole


def column_half(rows, side):
    width = rows.shape[1] // 2
    return lax.dynamic_slice_in_dim(rows, side * width, width, 1)


LANES = 2 * HEAD_DIM


def dot_rows(left_op, right_op):
    return lax.dot_general(
        left_op, right_op, (((1,), (1,)), ((), ())), preferred_element_type=jnp.float32
    )


def head_half(block, head):
    lanes = lax.broadcasted_iota(jnp.int32, block.shape, 1)
    return jnp.where((lanes >= HEAD_DIM) == (head == 1), block, jnp.zeros_like(block))


def pick_halves(first, second):
    lanes = lax.broadcasted_iota(jnp.int32, first.shape, 1)
    return jnp.where(lanes < HEAD_DIM, first, second)


def attend_kernel(lengths, query_ref, key_ref, value_ref, context_ref, probs_ref):
    length = lengths[pl.program_id(0)]
    size = query_ref.shape[0]
    query = query_ref[...]
    value = value_ref[...]
    key_at = lax.broadcasted_iota(jnp.int32, (size, size), 0)
    parts = []
    for head in range(2):
        scores = dot_rows(head_half(key_ref[...], head), query) * 0.125
        scores = jnp.where(key_at < length, scores, -1000000000.0)
        terms = jnp.exp(scores - jnp.max(scores, axis=0, keepdims=True))
        probs = (terms * (1.0 / jnp.sum(terms, axis=0, keepdims=True))).astype(jnp.bfloat16)
        probs_ref[pl.ds(head * size, size), :] = probs
        parts.append(project_left(probs, value))
    context_ref[...] = pick_halves(parts[0], parts[1]).astype(jnp.bfloat16)


def attend_back_kernel(
    query_ref, key_ref, value_ref, context_ref, probs_ref, grad_ref, *refs
):
    grad_query_ref, grad_key_ref, grad_value_ref = refs[-3:]
    size = query_ref.shape[0]
    query = query_ref[...]
    keys = key_ref[...]
    grad = grad_ref[...]
    both = grad.astype(jnp.float32) * context_ref[...].astype(jnp.float32)
    grads = ([], [], [])
    for head in range(2):
        shared = jnp.sum(head_half(both, head), axis=1, keepdims=True)
        shared = jnp.transpose(jnp.broadcast_to(shared, both.shape))[:1, :]
        probs = probs_ref[pl.ds(head * size, size), :]
        grad_probs = dot_rows(head_half(value_ref[...], head), grad)
        grad_scores = (probs.astype(jnp.float32) * (grad_probs - shared)).astype(jnp.bfloat16)
        grads[0].append(project_left(grad_scores, keys) * 0.125)
        grads[1].append(project(grad_scores, query) * 0.125)
        grads[2].append(project(probs, grad))
    for ref, pair in zip((grad_query_ref, grad_key_ref, grad_value_ref), grads):
        ref[...] = pick_halves(pair[0], pair[1]).astype(jnp.bfloat16)


def attend(queries, keys, values, lengths):
    slot_count = lengths.shape[0]
    size = queries.shape[0] // slot_count
    pairs = queries.shape[1] // LANES
    block = pl.BlockSpec((size, LANES), lambda slot, pair, lengths: (slot, pair))
    probs_block = pl.BlockSpec(
        (2 * size, size), lambda slot, pair, lengths: (slot * pairs + pair, 0)
    )
    return pl.pallas_call(
        attend_kernel,
        grid_spec=pltpu.PrefetchScalarGridSpec(
            num_scalar_prefetch=1,
            grid=(slot_count, pairs),
            in_specs=[block, block, block],
            out_specs=[block, probs_block],
        ),
        out_shape=[
            jax.ShapeDtypeStruct(queries.shape, jnp.bfloat16),
            jax.ShapeDtypeStruct((slot_count * pairs * 2 * size, size), jnp.bfloat16),
        ],
        name="attend",
        cost_estimate=pl.CostEstimate(
            flops=slot_count * pairs * 8 * size * size * LANES,
            transcendentals=slot_count * pairs * 2 * size * size,
            bytes_accessed=8 * queries.size + 4 * slot_count * pairs * size * size,
        ),
    )(lengths, queries, keys, values)


def attend_back(queries, keys, values, context, probs, grad_context, slot_count, span, held):
    first_pair, pair_count = span
    size = queries.shape[0] // slot_count
    pairs = queries.shape[1] // LANES
    block = pl.BlockSpec((size, LANES), lambda slot, pair: (slot, first_pair + pair))
    probs_block = pl.BlockSpec(
        (2 * size, size), lambda slot, pair: (slot * pairs + first_pair + pair, 0)
    )
    anywhere = pl.BlockSpec(memory_space=pl.ANY)
    return pl.pallas_call(
        attend_back_kernel,
        grid=(slot_count, pair_count),
        in_specs=[block, block, block, block, probs_block, block] + [anywhere] * len(held),
        out_specs=[block, block, block],
        out_shape=[jax.ShapeDtypeStruct(queries.shape, jnp.bfloat16)] * 3,
        input_output_aliases={6 + i: i for i in range(len(held))},
        name="attend_back",
        cost_estimate=pl.CostEstimate(
            flops=slot_count * pair_count * 16 * size * size * LANES,
            transcendentals=0,
            bytes_accessed=14 * size * LANES * slot_count * pair_count
            + 4 * slot_count * pair_count * size * size,
        ),
    )(queries, keys, values, context, probs, grad_context, *held)


PIECES = 3


def per_device(
    tokens,
    query_weight,
    key_weight,
    value_weight,
    output_weight,
    expand_weight,
    contract_weight,
    query_bias,
    value_bias,
    output_bias,
    first_gain,
    first_shift,
    expand_bias,
    contract_bias,
    second_gain,
    second_shift,
    cotangent,
    lengths,
    counts,
):
    slot_count = lengths.shape[0]
    row_count = tokens.shape[0]
    passage_len = row_count // slot_count
    features = tokens.shape[1]
    wide = expand_weight.shape[1]
    head_count = features // HEAD_DIM
    positions = jnp.arange(passage_len, dtype=jnp.int32)
    key_live = positions[None, :] < lengths[:, None]
    slot_live = jnp.arange(slot_count, dtype=jnp.int32) < counts[0]
    live_rows = (key_live & slot_live[:, None]).astype(jnp.float32).reshape(row_count, 1)
    queries = (project(tokens, query_weight) + query_bias).astype(jnp.bfloat16)
    key_rows = project(tokens, key_weight).astype(jnp.bfloat16)
    values = (project(tokens, value_weight) + value_bias).astype(jnp.bfloat16)
    context, probs = attend(queries, key_rows, values, lengths)
    attended = project(context, output_weight) + output_bias
    first_out, first_normed, first_inverse = norm_rows(
        tokens.astype(jnp.float32) + attended, first_gain, first_shift
    )
    first_low = first_out.astype(jnp.bfloat16)
    hidden = project(first_low, expand_weight) + expand_bias
    normal_cdf = 0.5 * (1.0 + jax.scipy.special.erf(hidden * 0.7071067811865476))
    active = (hidden * normal_cdf).astype(jnp.bfloat16)
    second = project(active, contract_weight) + contract_bias
    output_rows, second_normed, second_inverse = norm_rows(
        first_out + second, second_gain, second_shift
    )
    states = (output_rows * live_rows).astype(jnp.bfloat16)
    grad_out = cotangent.astype(jnp.float32) * live_rows
    grad_second, grad_second_gain, grad_second_shift = norm_back(
        grad_out, second_normed, second_inverse, second_gain
    )
    second_low = grad_second.astype(jnp.bfloat16)
    grad_contract_bias = jnp.sum(second_low.astype(jnp.float32), 0)
    core = my_side(0)
    contract_sent = project_left(column_half(active, 1 - core), second_low)
    contract_kept = project_left(column_half(active, core), second_low)
    contract_held = halve((contract_kept, swap(contract_sent, 0)), 1)[0]
    grad_active = project_right(second_low, contract_weight)
    density = jnp.exp(-0.5 * hidden * hidden) * 0.3989422804014327
    grad_hidden_low = (grad_active * (normal_cdf + hidden * density)).astype(jnp.bfloat16)
    contract_held = halve(contract_held, 2)[0]
    grad_expand_bias = jnp.sum(grad_hidden_low.astype(jnp.float32), 0)
    expand_sent = project_left(column_half(first_low, 1 - core), grad_hidden_low)
    expand_kept = project_left(column_half(first_low, core), grad_hidden_low)
    expand_held = (expand_kept, swap(expand_sent, 0))
    grad_first = grad_second + project_right(grad_hidden_low, expand_weight)
    grad_attended, grad_first_gain, grad_first_shift = norm_back(
        grad_first, first_normed, first_inverse, first_gain
    )
    attended_low = grad_attended.astype(jnp.bfloat16)
    attended_low, *expand_held = gate(attended_low, *expand_held)
    expand_held = halve(expand_held, 1)[0]
    grad_output_bias = jnp.sum(attended_low.astype(jnp.float32), 0)
    grad_context = project_right(attended_low, output_weight).astype(jnp.bfloat16)
    held = ()
    for piece in range(PIECES):
        count = head_count // 2 // PIECES
        if piece == PIECES - 1:
            *held, contract_kept, contract_swapped = gate(*held, *contract_held)
            contract_block = reduce_rest((contract_kept, contract_swapped), 3)
        held = attend_back(
            queries,
            key_rows,
            values,
            context,
            probs,
            grad_context,
            slot_count,
            (piece * count, count),
            held,
        )
    grad_queries, grad_keys, grad_values, *expand_held = gate(*held, *expand_held)
    expand_block = reduce_rest(expand_held, 2)
    grad_query_bias = jnp.sum(grad_queries.astype(jnp.float32), 0)
    grad_value_bias = jnp.sum(grad_values.astype(jnp.float32), 0)
    grad_tokens = (
        grad_attended
        + project_right(grad_queries, query_weight)
        + project_right(grad_keys, key_weight)
        + project_right(grad_values, value_weight)
    )
    small = jnp.concatenate(
        [
            grad_query_bias,
            grad_value_bias,
            grad_output_bias,
            grad_first_gain,
            grad_first_shift,
            grad_expand_bias,
            grad_contract_bias,
            grad_second_gain,
            grad_second_shift,
        ]
    )
    small_rows = small.shape[0] // wide
    small = jnp.pad(small.reshape(small_rows, wide), ((0, -small_rows % 8), (0, 0)))
    attn_parts = []
    for side, more in ((1 - core, [small]), (core, [])):
        token_half = column_half(tokens, side)
        block = jnp.concatenate(
            [
                project_left(token_half, part)
                for part in (grad_queries, grad_keys, grad_values)
            ]
            + [project_left(column_half(context, side), attended_low)],
            1,
        )
        attn_parts.append(jnp.concatenate([block] + more, 0))
    attn_held = (attn_parts[1], swap(attn_parts[0], 0))
    attn_block, small = reduce_rest(attn_held, 1, small)
    smalls = small[:small_rows].reshape(-1)
    contract_whole = assemble(spread(contract_block, wide), wide)
    expand_whole = assemble(spread(expand_block, features), features)
    attn_pieces = spread(attn_block, features)
    attn_mats = [
        assemble(
            [(at, part[:, i * features : (i + 1) * features]) for at, part in attn_pieces], features
        )
        for i in range(4)
    ]
    attn_small = [smalls[i * features : (i + 1) * features] for i in range(5)]
    tail = 5 * features + wide
    ffn_small = [smalls[5 * features : tail]] + [
        smalls[tail + i * features : tail + (i + 1) * features] for i in range(3)
    ]
    return (
        states,
        grad_tokens,
        attn_mats[0],
        attn_mats[1],
        attn_mats[2],
        attn_mats[3],
        expand_whole,
        contract_whole,
        attn_small[0],
        attn_small[1],
        attn_small[2],
        attn_small[3],
        attn_small[4],
        ffn_small[0],
        ffn_small[1],
        ffn_small[2],
        ffn_small[3],
    )


def solution(mesh):
    placed = (
        P(("dp", "rep"), None),
        P(),
        P(),
        P(),
        P(),
        P(),
        P(),
        P(),
        P(),
        P(),
        P(),
        P(),
        P(),
        P(),
        P(),
        P(),
        P(("dp", "rep"), None),
        P(("dp", "rep")),
        P(("dp", "rep")),
    )
    return jax.shard_map(
        per_device,
        mesh=mesh,
        in_specs=placed,
        out_specs=(
            P(("dp", "rep"), None),
            P(("dp", "rep"), None),
            P(),
            P(),
            P(),
            P(),
            P(),
            P(),
            P(),
            P(),
            P(),
            P(),
            P(),
            P(),
            P(),
            P(),
            P(),
        ),
        check_vma=False,
    )
```
